32 devices in a mesh: frame: 4 (over y, core), expert: 8 (over z, x).
Axes of the slice: x: 2, y: 2, z: 4, core: 2. Of those that a mesh axis runs over, the one named last changes fastest.
Arguments:
- frames: bfloat16 [8, 4096, 1408], P('expert', 'frame'), may hold values from -16 to 16
- frame_counts: int32 [8], P('expert'), may hold values from 1 to 16, as said below
- latents: bfloat16 [32, 1408], replicated, may hold values from -36 to 36
- w_kv: bfloat16 [1408, 2816], P('expert'), may hold values from -0.15625 to 0.15625
- w_proj: bfloat16 [1408, 6144], P('expert', 'frame'), may hold values from -0.15625 to 0.15625
- norm_gain: bfloat16 [6144], replicated, may hold values from 0.099609375 to 1.8984375
- router: bfloat16 [6144, 8], replicated, may hold values from -0.078125 to 0.078125
- expert_ids: int32 [256, 2], P('expert'), may hold values from 0 to 7, all different within a row; in each aligned block of 32 rows (0 to 31, 32 to 63, ...) at most 16 rows name the same one
- w_gate: bfloat16 [8, 6144, 8192], P('expert', None, 'frame'), may hold values from -0.078125 to 0.078125
- w_up: bfloat16 [8, 6144, 8192], P('expert', None, 'frame'), may hold values from -0.078125 to 0.078125
- w_down: bfloat16 [8, 8192, 6144], P('expert', 'frame'), may hold values from -0.25 to 0.25
Outputs:
- layer_out: bfloat16 [256, 6144], P('expert', 'frame')
The draws below stay inside these ranges and needn't reach their ends.
Inputs may be any that keep to these rules, and one draw needn't show every extreme that they name: `frame_counts`: some clip has all 16 frames valid and some other clip exactly one. `expert_ids`: each row names two different experts. Within the 32 rows of one index of expert no expert is named by more than 16 rows, and in some of these blocks one expert is named by exactly 16.
All inputs are finite; a program needn't handle non-finite values.
Results may differ from the reference program's by a relative error of at most 0.022.
Values may be sent and summed in bfloat16 or wider, within the bound.
No kernel may reach another device: no remote copies, remote signals or barrier semaphores. Data moves between devices by JAX's collectives and lax.ppermute only.
A program may use at most 192 MiB of HBM per device.

```python
import math
from functools import partial
import jax
import jax.numpy as jnp
import numpy as np
from jax import lax

V = 1408
HEADS = 16
HEAD = 88
LAT = 32
PATCH = 256
D = 6144
FFH = 8192
EXPERTS = 8
SH = 1
FH_DEV = 2048
TOK_DEV = 32
CAP = 16
CLIPS = 8
FRAMES = 16
TOKENS = 256
N_FRAME = 4
N_EXPERT = 8


def draw_frame_counts(key, part):
    key_counts, key_long, key_offset = jax.random.split(key, 3)
    counts = jax.random.randint(key_counts, (CLIPS,), 1, FRAMES + 1, dtype=jnp.int32)
    longest = jax.random.randint(key_long, (), 0, CLIPS, dtype=jnp.int32)
    offset = jax.random.randint(key_offset, (), 1, CLIPS, dtype=jnp.int32)
    shortest = (longest + offset) % CLIPS
    counts = counts.at[longest].set(FRAMES)
    return counts.at[shortest].set(1)


def draw_frames(key, part):
    key_base = jax.random.fold_in(key, 0)
    dims_all = (CLIPS, FRAMES * PATCH, V)
    return jnp.clip(jax.random.normal(key_base, dims_all, jnp.float32), -8.0, 8.0).astype(jnp.bfloat16)


def draw_latents(key, part):
    key_base = jax.random.fold_in(key, 0)
    base = jax.random.normal(key_base, (LAT, V), jnp.float32)
    return jnp.clip(base * 1.5, -8.0, 8.0).astype(jnp.bfloat16)


def steps_of(stream_key, dims, shards, smallest, largest):
    level, own = 1.0, jax.random.fold_in(stream_key, 6)
    for axis_at, parts in shards:
        heights = jnp.exp(jax.random.uniform(jax.random.fold_in(own, axis_at), (parts,), jnp.float32, smallest / len(shards), largest / len(shards)))
        level = level * jnp.repeat(heights, dims[axis_at] // parts).reshape([-1 if axis == axis_at else 1 for axis in range(len(dims))])
    return level


def shared_out(rng, own, number, rows, amount, top, reach, slope):
    ranking = jax.random.permutation(rng, amount)
    crowded, usual = shares(amount, rows * top, reach, slope, True), shares(amount, rows * top, reach, slope, False)
    places = jnp.arange(amount)

    def named(sizes, turn):
        used = int((sizes > 0).sum())
        fixed = max(1, used // 4)
        moved = fixed + (places - fixed + turn * (used - fixed)) % max(1, amount - fixed)
        return jnp.zeros((amount,), jnp.int32).at[ranking[jnp.where(places < fixed, places, moved)]].set(jnp.asarray(sizes, jnp.int32))

    sizes = jnp.where(number % 4 == 0, named(crowded, number // 4), named(usual, number - number // 4 - 1))
    mixed = jax.random.permutation(jax.random.fold_in(own, 3), amount)
    donor, sink = mixed[0:amount // 2 * 2:2], mixed[1:amount // 2 * 2:2]
    margin = jnp.minimum(sizes[donor] - 1, reach - sizes[sink]) // 2
    margin = jnp.where((donor == ranking[0]) | (sink == ranking[0]) | (sizes[sink] == 0), 0, jnp.maximum(margin, 0))
    moved = jax.random.randint(jax.random.fold_in(own, 4), (amount // 2,), 0, 1 << 20) % (margin + 1)
    sizes = sizes.at[donor].add(-moved).at[sink].add(moved)
    items = jnp.searchsorted(jnp.cumsum(sizes), jnp.arange(rows * top), side="right").astype(jnp.int32)
    listing = items.reshape(top, rows).T
    listing = listing[jax.random.permutation(jax.random.fold_in(own, 1), rows)]
    turn = jax.random.randint(jax.random.fold_in(own, 2), (rows, 1), 0, top)
    return jnp.take_along_axis(listing, (jnp.arange(top)[None, :] + turn) % top, axis=1)


def shares(count, total, bound, skew, full):
    weights = [(1 << 20) // math.isqrt(grade ** skew) + 1 for grade in range(1, count + 1)]
    largest = bound if full else min(bound, max(-(-total // count), total * weights[0] // sum(weights)))
    least = 1 if total - largest >= count - 1 else 0
    given, spare = [largest] + [least] * (count - 1), total - largest - least * (count - 1)
    while spare > 0:
        movable = [i for i in range(1, count) if given[i] < largest] or [i for i in range(1, count) if given[i] < bound]
        mass, left = sum([weights[i] for i in movable]), spare
        for i in movable:
            addition = min(bound - given[i], max(1, left * weights[i] // mass), spare)
            given[i] = given[i] + addition
            spare = spare - addition
    return np.array(given)


def gaussian(rng, dims, deviation, reach, pieces=(), kind=jnp.bfloat16):
    entries = deviation * jax.random.normal(rng, dims, jnp.float32)
    if pieces:
        entries = entries * steps_of(rng, dims, pieces, -0.22, 0.18)
    return jnp.clip(entries, -reach, reach).astype(kind)


def setup_inputs(seed: int = 0) -> dict:
    key_of = jax.random.split(jax.random.key(seed), 12)
    frames = draw_frames(jax.random.fold_in(key_of[11], 71), 0)
    frame_counts = draw_frame_counts(jax.random.fold_in(key_of[11], 71), 0)
    latents = draw_latents(jax.random.fold_in(key_of[11], 71), 0)
    w_kv = gaussian(key_of[3], (V, 2 * V), V ** -0.5, 0.15625, ((0, 8),))
    w_proj = gaussian(key_of[4], (V, D), V ** -0.5, 0.15625, ((0, 8), (1, 4)))
    norm_gain = jnp.clip(1.0 + 0.18 * jax.random.normal(key_of[5], (D,), jnp.float32), 0.099609375, 1.8984375).astype(jnp.bfloat16)
    router = gaussian(key_of[6], (D, EXPERTS), D ** -0.5, 0.078125)
    expert_ids_keys = jax.random.split(jax.random.fold_in(key_of[7], 1), TOKENS // TOK_DEV)
    expert_ids_turns = jax.random.permutation(jax.random.fold_in(key_of[7], 3), TOKENS // TOK_DEV)
    expert_ids = jax.vmap(lambda own, number: shared_out(jax.random.fold_in(key_of[7], 2), own, number, TOK_DEV, EXPERTS, 2, CAP, 2))(expert_ids_keys, expert_ids_turns).reshape((TOKENS, 2))
    w_gate = gaussian(key_of[8], (EXPERTS * SH, D, FFH // SH), D ** -0.5, 0.078125, ((0, 8), (2, 4)))
    w_up = gaussian(key_of[9], (EXPERTS * SH, D, FFH // SH), D ** -0.5, 0.078125, ((0, 8), (2, 4)))
    w_down = gaussian(key_of[10], (EXPERTS * SH, FFH // SH, D), (FFH // 16) ** -0.5, 0.25, ((0, 8), (1, 4)))
    return dict(frames=frames, frame_counts=frame_counts, latents=latents, w_kv=w_kv, w_proj=w_proj, norm_gain=norm_gain, router=router, expert_ids=expert_ids, w_gate=w_gate, w_up=w_up, w_down=w_down)


NEG_BIG = -1e+30
EPSILON = 1e-05

def pool_clip(inputs, latents, w_kv):
    clip_frames, valid_count = inputs
    key_value = jnp.dot(clip_frames, w_kv, preferred_element_type=jnp.float32).astype(jnp.bfloat16)
    key_rows = key_value[:, :V].astype(jnp.float32).reshape(-1, HEADS, HEAD)
    value_rows = key_value[:, V:].astype(jnp.float32).reshape(-1, HEADS, HEAD)
    queries = latents.astype(jnp.float32).reshape(LAT, HEADS, HEAD)
    scores = jnp.einsum('lhd,phd->hlp', queries, key_rows) / math.sqrt(HEAD)
    frame_of = jnp.arange(key_rows.shape[0], dtype=jnp.int32) // PATCH
    valid = frame_of < valid_count
    masked = jnp.where(valid, scores, NEG_BIG)
    peak = lax.optimization_barrier(jnp.max(masked, axis=-1, keepdims=True))
    expos = jnp.where(valid, jnp.exp(masked - peak), 0.0)
    totals = lax.optimization_barrier(jnp.sum(expos, axis=-1))
    summed = jnp.einsum('hlp,phd->lhd', expos, value_rows)
    pooled = summed / jnp.transpose(totals)[:, :, None]
    return pooled.reshape(LAT, V).astype(jnp.bfloat16)

def expert_rows(expert, normed, pair_expert, pair_row, pair_token, w_gate, w_up, w_down):
    slot_total = N_EXPERT * CAP
    target = jnp.where(pair_expert == expert, pair_row, slot_total).astype(jnp.int32)
    token_of = jnp.full((slot_total + 1,), TOKENS, jnp.int32).at[target].set(pair_token)[:slot_total]
    padded = jnp.concatenate([normed, jnp.zeros((1, D), normed.dtype)], axis=0)
    inputs = padded[token_of]
    gate_cols = jnp.moveaxis(w_gate.reshape(EXPERTS, SH, D, FFH // SH)[expert], 0, 1).reshape(D, FFH)
    up_cols = jnp.moveaxis(w_up.reshape(EXPERTS, SH, D, FFH // SH)[expert], 0, 1).reshape(D, FFH)
    gate_val = jnp.dot(inputs, gate_cols, preferred_element_type=jnp.float32)
    up_val = jnp.dot(inputs, up_cols, preferred_element_type=jnp.float32)
    hidden = (jax.nn.silu(gate_val) * up_val).astype(jnp.bfloat16).reshape(slot_total, SH, N_FRAME, FH_DEV)
    down_blocks = w_down.reshape(EXPERTS, SH, N_FRAME, FH_DEV, D)[expert]

    def shard_sum(shard):

        def add_block(block, running):
            part = jnp.dot(hidden[:, shard, block], down_blocks[shard, block], preferred_element_type=jnp.float32).astype(jnp.bfloat16)
            part = lax.optimization_barrier(part)
            return running + part.astype(jnp.float32)
        merged = lax.fori_loop(0, N_FRAME, add_block, jnp.zeros((slot_total, D), jnp.float32))
        return merged.astype(jnp.bfloat16)
    shard_out = lax.map(shard_sum, jnp.arange(SH, dtype=jnp.int32))
    return lax.optimization_barrier(jnp.sum(shard_out.astype(jnp.float32), axis=0))

def reference(frames, frame_counts, latents, w_kv, w_proj, norm_gain, router, expert_ids, w_gate, w_up, w_down):
    pooled = lax.map(partial(pool_clip, latents=latents, w_kv=w_kv), (frames, frame_counts))
    pooled = pooled.reshape(TOKENS, V)
    projected = jnp.dot(pooled, w_proj, preferred_element_type=jnp.float32).astype(jnp.bfloat16)
    x_float = projected.astype(jnp.float32)
    gain_all = norm_gain.astype(jnp.float32)
    scale = lax.rsqrt(lax.optimization_barrier(jnp.mean(x_float * x_float, axis=-1)) + EPSILON)
    normed = (x_float * scale[:, None] * gain_all).astype(jnp.bfloat16)
    logits = jnp.dot(x_float * gain_all, router.astype(jnp.float32), precision=lax.Precision.HIGHEST) * scale[:, None]
    chosen = jnp.take_along_axis(logits, expert_ids, axis=1)
    gates = jax.nn.softmax(chosen, axis=-1)
    ids_block = expert_ids.reshape(N_EXPERT, TOK_DEV * 2)
    onehot = (ids_block[:, :, None] == jnp.arange(EXPERTS, dtype=jnp.int32)[None, None, :]).astype(jnp.int32)
    before = (jnp.cumsum(onehot, axis=1) - onehot).astype(jnp.int32)
    position = lax.optimization_barrier(jnp.sum(before * onehot, axis=-1)).astype(jnp.int32)
    pair_row = (jnp.arange(N_EXPERT, dtype=jnp.int32)[:, None] * CAP + position).reshape(-1).astype(jnp.int32)
    pair_expert = expert_ids.reshape(-1).astype(jnp.int32)
    pair_token = (jnp.arange(TOKENS * 2, dtype=jnp.int32) // 2).astype(jnp.int32)
    results = lax.map(partial(expert_rows, normed=normed, pair_expert=pair_expert, pair_row=pair_row, pair_token=pair_token, w_gate=w_gate, w_up=w_up, w_down=w_down), jnp.arange(EXPERTS, dtype=jnp.int32))
    pair_out = results[pair_expert, pair_row].reshape(TOKENS, 2, D)
    moe_out = lax.optimization_barrier(jnp.sum(pair_out * gates[:, :, None], axis=1))
    return (x_float + moe_out).astype(jnp.bfloat16)
```

```python
import math

import jax
import jax.numpy as jnp
from jax import lax
from jax.experimental import pallas as pl
from jax.experimental.pallas import tpu as pltpu
from jax.sharding import PartitionSpec as P

HEADS = 16
PATCH = 256


NEG_BIG = -1e30
EPSILON = 1e-05


def joined(value, axis, join):
    pieces = jax.tree.map(lambda part: lax.all_gather(part, axis), value)
    head = jax.tree.map(lambda part: part[0], pieces)
    tail = jax.tree.map(lambda part: part[1:], pieces)
    subtotal, _ = lax.scan(lambda subtotal, piece: (join(subtotal, piece), None), head, tail)
    return subtotal


def rescale(weighted, factor):
    return (weighted.reshape(factor.shape + (-1,)) * factor[..., None]).reshape(weighted.shape)


def combine_parts(earlier, later):
    peak_left, totals_left, weighted_left = earlier
    peak_right, totals_right, weighted_right = later
    peak_both = jnp.maximum(peak_left, peak_right)
    factor_left = jnp.exp(peak_left - peak_both)
    factor_right = jnp.exp(peak_right - peak_both)
    totals_both = totals_left * factor_left + totals_right * factor_right
    weighted_both = rescale(weighted_left, factor_left) + rescale(weighted_right, factor_right)
    return (peak_both, totals_both, weighted_both)


def local(
    frames, frame_counts, latents, w_kv, w_proj, norm_gain, router, expert_ids, w_gate, w_up, w_down
):
    clip_count, frame_tokens, width = frames.shape
    head_count = HEADS
    head_size = width // head_count
    latent_count = latents.shape[0]
    tokens_here = clip_count * latent_count
    flat_frames = frames.reshape(clip_count * frame_tokens, width)
    columns = flat_frames
    kv_sum = jnp.dot(
        columns,
        lax.all_gather(w_kv, "expert", axis=0, tiled=True),
        preferred_element_type=jnp.float32,
    )
    key_value = kv_sum.astype(jnp.bfloat16).reshape(clip_count, frame_tokens, 2 * width)
    key_rows = key_value[:, :, :width].reshape(clip_count, frame_tokens, head_count, head_size)
    value_rows = key_value[:, :, width:].reshape(clip_count, frame_tokens, head_count, head_size)
    queries = latents.reshape(latent_count, head_count, head_size)
    scores = jnp.einsum(
        "lhd,cphd->clhp", queries, key_rows, preferred_element_type=jnp.float32
    ) / math.sqrt(head_size)
    frames_here = frame_tokens // PATCH
    frame_of = (
        lax.axis_index("frame") * frames_here + jnp.arange(frame_tokens, dtype=jnp.int32) // PATCH
    )
    valid = (frame_of[None, :] < frame_counts[:, None])[:, None, None, :]
    masked = jnp.where(valid, scores, NEG_BIG)
    peak = jnp.max(masked, axis=-1)
    expos = jnp.where(valid, jnp.exp(masked - peak[..., None]), 0.0)
    totals = jnp.sum(expos, axis=-1)
    weighted = jnp.einsum("clhp,cphd->clhd", expos, value_rows, preferred_element_type=jnp.float32)
    weighted = weighted.reshape(clip_count, latent_count, width)
    peak_all, totals_all, weighted_all = joined((peak, totals, weighted), "frame", combine_parts)
    pooled = (
        rescale(weighted_all, 1.0 / totals_all).reshape(tokens_here, width).astype(jnp.bfloat16)
    )
    columns = pooled
    x_part = jnp.dot(
        columns,
        lax.all_gather(w_proj, "expert", axis=0, tiled=True),
        preferred_element_type=jnp.float32,
    ).astype(jnp.bfloat16)
    part_width = w_proj.shape[1]
    model_width = router.shape[0]
    gain_all = norm_gain.astype(jnp.float32)
    router_all = router.astype(jnp.float32)
    x_float = x_part.astype(jnp.float32)
    x_whole = lax.all_gather(x_part, "frame", axis=1, tiled=True).astype(jnp.float32)
    squares = jnp.sum(x_whole * x_whole, axis=-1)
    raw_logits = jnp.dot(x_whole * gain_all, router_all, precision=lax.Precision.HIGHEST)
    scale = lax.rsqrt(squares / model_width + EPSILON)
    normed = (x_whole * scale[:, None] * gain_all).astype(jnp.bfloat16)
    logits = raw_logits * scale[:, None]
    chosen = jnp.take_along_axis(logits, expert_ids, axis=1)
    gates = jax.nn.softmax(chosen, axis=-1)
    expert_total = router.shape[1]
    capacity = tokens_here // 2
    pair_ids = expert_ids.reshape(-1)
    onehot = (pair_ids[:, None] == jnp.arange(expert_total, dtype=jnp.int32)[None, :]).astype(
        jnp.int32
    )
    earlier_hits = jnp.cumsum(onehot, axis=0) - onehot
    position = jnp.sum(earlier_hits * onehot, axis=-1)
    slot_of = pair_ids * capacity + position
    pair_hit = (
        slot_of[None, :] == jnp.arange(expert_total * capacity, dtype=jnp.int32)[:, None]
    ).astype(jnp.float32)
    select = pair_hit.reshape(-1, tokens_here, 2).sum(-1).astype(jnp.bfloat16)
    mixing = (pair_hit * gates.reshape(-1)[None, :]).reshape(-1, tokens_here, 2).sum(-1)
    packed = jnp.dot(select, normed, preferred_element_type=jnp.float32).astype(jnp.bfloat16)
    shard_count = lax.axis_size("expert") // expert_total
    row_width = packed.shape[1]
    send_rows = jnp.broadcast_to(
        packed.reshape(expert_total, 1, capacity, row_width),
        (expert_total, shard_count, capacity, row_width),
    )
    send_rows = send_rows.reshape(expert_total * shard_count, capacity, row_width)
    gate_local = w_gate[0]
    up_local = w_up[0]
    down_local = w_down[0]
    arrived = lax.all_to_all(send_rows, "expert", split_axis=0, concat_axis=0, tiled=True)
    flat_rows = arrived.reshape(-1, arrived.shape[-1])
    gate_val = jnp.dot(flat_rows, gate_local, preferred_element_type=jnp.float32)
    up_val = jnp.dot(flat_rows, up_local, preferred_element_type=jnp.float32)
    hidden_rows = (jax.nn.silu(gate_val) * up_val).astype(jnp.bfloat16)
    hidden = hidden_rows.reshape(arrived.shape[0], arrived.shape[1], -1)
    slot_rows = hidden.reshape(-1, hidden.shape[-1])
    columns = down_local
    summed = lax.psum_scatter(
        lax.dot_general(
            columns, slot_rows, (((0,), (1,)), ((), ())), preferred_element_type=jnp.float32
        ).astype(jnp.bfloat16),
        "frame",
        scatter_dimension=0,
        tiled=True,
    )
    outgoing = summed.reshape(part_width, -1, capacity)
    returned = lax.all_to_all(outgoing, "expert", split_axis=1, concat_axis=1, tiled=True)
    per_expert = (
        returned.astype(jnp.float32).reshape(part_width, expert_total, shard_count, capacity).sum(2)
    )
    per_expert = per_expert.reshape(part_width, expert_total * capacity)
    moe_part = jnp.dot(per_expert, mixing, precision=lax.Precision.HIGHEST)
    return (x_float + jnp.transpose(moe_part)).astype(jnp.bfloat16)


def swap(value, axis, bits, size):
    return lax.ppermute(value, axis, [(i, i ^ bits) for i in range(size)])


def after(value, *earlier):
    return lax.optimization_barrier((value, *earlier))[0]


PIECES = (
    tuple((2 * d, 0) for d in range(4)),
    tuple((2 * d + 1, 0) for d in range(4)),
    tuple((2 * d, 2) for d in range(4)),
    tuple((2 * d + 1, 2) for d in (0, 1)),
    tuple((2 * d + 1, 2) for d in (2, 3)),
)
PLACES = tuple(places for group in PIECES for places in (group, tuple((e, f + 1) for e, f in group)))


def along_z(piece):
    return jnp.stack([piece] + [swap(piece, "expert", 2 * d, 8) for d in (1, 2, 3)])


def spread(column, *earlier):
    core = lambda value: swap(value, "frame", 1, 4)
    by_x = swap(column, "expert", 1, 8)
    by_y = swap(column, "frame", 2, 4)
    low = swap(by_y[:2], "expert", 1, 8)
    high = swap(by_x[2:], "frame", 2, 4)
    groups = []
    for value in (column, by_x, by_y, low, high):
        groups += [value, core(value)]
    return groups, (low, high, by_x)


def place_pieces(where, pieces, whole):
    rows = pieces[0].shape[1]
    for places, piece in zip(PLACES, pieces):
        for at, (e_bits, f_bits) in enumerate(places):
            row = pl.multiple_of((where[0] ^ e_bits) * rows, 16)
            whole[where[1] ^ f_bits, pl.ds(row, rows), :] = piece[at]


def attend_body(where, frames, *refs):
    pieces, (pooled_frames, states, whole) = refs[: len(PLACES)], refs[len(PLACES) :]
    place_pieces(where, pieces, whole)
    tokens = frames.shape[0]
    row = lax.broadcasted_iota(jnp.int32, (tokens, whole.shape[2]), 0)
    valid = row < where[2]
    for group in range(whole.shape[0]):
        scores = jnp.dot(frames[...], whole[group], preferred_element_type=jnp.float32)
        masked = jnp.where(valid, scores, NEG_BIG)
        peak = jnp.max(masked, axis=0, keepdims=True)
        expos = jnp.where(valid, jnp.exp(masked - peak), 0.0)
        total = jnp.sum(expos, axis=0, keepdims=True)
        some = total > 0.0
        safe = jnp.where(some, total, 1.0)
        weights = (expos * (1.0 / safe)).astype(jnp.bfloat16)
        states[pl.ds(group, 1), :] = jnp.where(some, peak + jnp.log(safe), NEG_BIG)
        pooled_frames[group] = lax.dot_general(
            weights, frames[...], (((0,), (0,)), ((), ())), preferred_element_type=jnp.float32
        ).astype(jnp.bfloat16)


def values_body(where, pooled_frames, states, *refs):
    pieces, (packed, whole) = refs[: len(PLACES)], refs[len(PLACES) :]
    place_pieces(where, pieces, whole)
    groups, pairs, _ = pooled_frames.shape
    width = whole.shape[2]
    head_size = width // 4
    latents = pairs // 4
    head_of = lax.broadcasted_iota(jnp.int32, (latents, width), 1) // head_size
    for group in range(groups):
        every = jnp.dot(pooled_frames[group], whole[group], preferred_element_type=jnp.float32)
        own = jnp.zeros((latents, width), jnp.float32)
        for head in range(4):
            own = jnp.where(head_of == head, every[head * latents : (head + 1) * latents, :], own)
        start = group * 384
        packed[:, start : start + width] = own.astype(jnp.bfloat16)
        packed[:, start + width : start + 384] = states[group]


def combine_body(where, parts, pooled):
    latents = parts.shape[1]
    width = 352
    head_size = width // 4
    head_of = lax.broadcasted_iota(jnp.int32, (latents, width), 1) // head_size
    for turn in range(4):
        start = pl.multiple_of((where[0] ^ turn) * 384, 128)
        logs, values = [], []
        for part in range(4):
            block = parts[part, :, pl.ds(start, 384)].astype(jnp.float32)
            state = block[:, width : width + 4] + block[:, width + 4 : width + 8]
            state = state + block[:, width + 8 : width + 12]
            logs.append(state)
            values.append(block[:, :width])
        peak = jnp.maximum(jnp.maximum(logs[0], logs[1]), jnp.maximum(logs[2], logs[3]))
        shares = [jnp.exp(state - peak) for state in logs]
        inverse = 1.0 / (shares[0] + shares[1] + shares[2] + shares[3])
        joined_up = jnp.zeros((latents, width), jnp.float32)
        for share, value in zip(shares, values):
            share = share * inverse
            spread_out = jnp.zeros((latents, width), jnp.float32)
            for head in range(4):
                spread_out = jnp.where(head_of == head, share[:, head : head + 1], spread_out)
            joined_up = joined_up + value * spread_out
        pooled[turn] = jnp.zeros((latents, 384), jnp.bfloat16)
        pooled[turn, :, :width] = joined_up.astype(jnp.bfloat16)


def enter_body(where, own, other, gain, gate_w, up_w, gate_out, up_out, squares):
    turn, step = pl.program_id(0), pl.program_id(1)
    depth = gate_w.shape[1]

    @pl.when((turn == 0) & (step == 0))
    def _():
        gate_out[...] = jnp.zeros_like(gate_out)
        up_out[...] = jnp.zeros_like(up_out)
        squares[...] = jnp.zeros_like(squares)

    def add(rows):
        block = rows[:, pl.ds(pl.multiple_of(step * depth, 128), depth)].astype(jnp.float32)
        total = jnp.sum(block * block, axis=1, keepdims=True)
        squares[...] += jnp.broadcast_to(total, squares.shape)
        gained = (block * gain[0].astype(jnp.float32)).astype(jnp.bfloat16)
        gate_out[...] += jnp.dot(gained, gate_w[0], preferred_element_type=jnp.float32)
        up_out[...] += jnp.dot(gained, up_w[0], preferred_element_type=jnp.float32)

    pl.when(turn == 0)(lambda: add(own))
    pl.when(turn == 1)(lambda: add(other))


def near_body(where, own, other, gain, gate_w, up_w, gate_out, up_out, squares):
    enter_body(where, own, other, gain, gate_w, up_w, gate_out, up_out, squares)


def far_body(where, own, other, gain, gate_w, up_w, gate_in, up_in, squares_in, hidden, gate_sum, up_sum, squares):
    enter_body(where, own, other, gain, gate_w, up_w, gate_sum, up_sum, squares)

    @pl.when((pl.program_id(0) == 1) & (pl.program_id(1) == pl.num_programs(1) - 1))
    def _():
        width = gain.shape[2] * pl.num_programs(1) * 4
        mean = (squares[:, :1] + squares_in[:, :1]) / width
        scale = lax.rsqrt(mean + EPSILON)
        gate_val = (gate_sum[...] + gate_in[...]) * scale
        up_val = (up_sum[...] + up_in[...]) * scale
        hidden[...] = (gate_val / (1.0 + jnp.exp(-gate_val)) * up_val).astype(jnp.bfloat16)


def expert_in(where, own, other, gain, gate_w, up_w, bits, earlier=None):
    rows, columns = own.shape
    depth = 512
    steps = columns // depth
    hidden_width = gate_w.shape[2]
    whole = lambda shape: pl.BlockSpec(shape, lambda turn, step, where: (0, 0))
    chunk = lambda turn, step, where: (where[1] ^ (bits + turn)) * steps + step
    gain_spec = pl.BlockSpec((1, 1, depth), lambda turn, step, where: (chunk(turn, step, where), 0, 0))
    weight_spec = pl.BlockSpec((1, depth, hidden_width), lambda turn, step, where: (0, chunk(turn, step, where), 0))
    sums = [
        jax.ShapeDtypeStruct((rows, hidden_width), jnp.float32),
        jax.ShapeDtypeStruct((rows, hidden_width), jnp.float32),
        jax.ShapeDtypeStruct((rows, 128), jnp.float32),
    ]
    in_specs = [whole(own.shape), whole(other.shape), gain_spec, weight_spec, weight_spec]
    operands = [own, other, gain.reshape(-1, 1, depth), gate_w, up_w]
    if earlier is None:
        out_shape, out_specs, scratch, body = sums, [whole(s.shape) for s in sums], [], near_body
    else:
        out_shape = jax.ShapeDtypeStruct((rows, hidden_width), jnp.bfloat16)
        out_specs = whole(out_shape.shape)
        scratch = [pltpu.VMEM(s.shape, s.dtype) for s in sums]
        in_specs += [whole(s.shape) for s in sums]
        operands += list(earlier)
        body = far_body
    return pl.pallas_call(
        body,
        out_shape=out_shape,
        grid_spec=pltpu.PrefetchScalarGridSpec(
            num_scalar_prefetch=1, grid=(2, steps), in_specs=in_specs, out_specs=out_specs, scratch_shapes=scratch
        ),
        cost_estimate=cost(8 * rows * columns * hidden_width, 8 * columns * hidden_width),
    )(where, *operands)


def cost(flops, moved):
    return pl.CostEstimate(flops=flops, transcendentals=0, bytes_accessed=moved)


def down_body(where, hidden, weight, out):
    out[0] = jnp.dot(hidden[...], weight[0], preferred_element_type=jnp.float32).astype(jnp.bfloat16)


def expert_out(where, hidden, down_w, bits):
    rows, depth = hidden.shape
    part = down_w.shape[2] // 4
    width = 512
    steps = part // width
    return pl.pallas_call(
        down_body,
        out_shape=jax.ShapeDtypeStruct((2, rows, part), jnp.bfloat16),
        grid_spec=pltpu.PrefetchScalarGridSpec(
            num_scalar_prefetch=1,
            grid=(2, steps),
            in_specs=[
                pl.BlockSpec((rows, depth), lambda turn, step, where: (0, 0)),
                pl.BlockSpec(
                    (1, depth, width),
                    lambda turn, step, where: (0, 0, (where[1] ^ (bits + turn)) * steps + step),
                ),
            ],
            out_specs=pl.BlockSpec((1, rows, width), lambda turn, step, where: (turn, 0, step)),
        ),
        cost_estimate=cost(4 * rows * depth * part, 4 * depth * part),
    )(where, hidden, down_w)


def in_vmem(body, out_shape, scratch=()):
    space = lambda _: pl.BlockSpec(memory_space=pltpu.VMEM)

    def call(where, *operands):
        return pl.pallas_call(
            body,
            out_shape=out_shape,
            in_specs=[pl.BlockSpec(memory_space=pltpu.SMEM)] + [space(o) for o in operands],
            out_specs=jax.tree.map(space, out_shape),
            scratch_shapes=list(scratch),
        )(where, *operands)

    return call


def fast_local(
    frames, frame_counts, latents, w_kv, w_proj, norm_gain, router, expert_ids, w_gate, w_up, w_down
):
    _, frame_tokens, width = frames.shape
    latent_count = latents.shape[0]
    head_size = width // HEADS
    e, f = lax.axis_index("expert"), lax.axis_index("frame")
    rows = w_kv.shape[0]
    quarter = width // 4
    frames_here = frame_tokens // PATCH
    valid_tokens = jnp.clip((frame_counts[0] - f * frames_here) * PATCH, 0, frame_tokens)
    where = jnp.stack([e, f, valid_tokens]).astype(jnp.int32)

    head_here = f * 4 + jnp.arange(4, dtype=jnp.int32)
    head_of = jnp.arange(width, dtype=jnp.int32) // head_size
    spaced = jnp.where(
        head_here[:, None, None] == head_of[None, None, :], latents[None], jnp.zeros((), jnp.bfloat16)
    ).reshape(4 * latent_count, width)
    asked = lax.dot_general(
        w_kv[:, :width], spaced, (((1,), (1,)), ((), ())), preferred_element_type=jnp.float32
    )
    asked = (asked / math.sqrt(head_size)).astype(jnp.bfloat16)
    asked_column = along_z(asked)
    asked_pieces, asked_x = spread(asked_column)
    value_piece = lax.dynamic_slice(w_kv, (0, width + f * quarter), (rows, quarter))
    value_column = along_z(after(value_piece, asked_column))
    value_pieces, value_x = spread(after(value_column, *asked_x))
    proj_other = swap(after(w_proj, *value_x), "expert", 1, 8)

    pooled_frames, states = in_vmem(
        attend_body,
        (
            jax.ShapeDtypeStruct((4, 4 * latent_count, width), jnp.bfloat16),
            jax.ShapeDtypeStruct((4, 4 * latent_count), jnp.float32),
        ),
        [pltpu.VMEM((4, width, 4 * latent_count), jnp.bfloat16)],
    )(where, frames[0], *asked_pieces)
    by_latent = jnp.transpose(states.reshape(4, 4, latent_count), (0, 2, 1))
    high = lax.reduce_precision(by_latent, 8, 7)
    middle = lax.reduce_precision(by_latent - high, 8, 7)
    low = (by_latent - high) - middle
    blank = jnp.zeros((4, latent_count, 20), jnp.float32)
    state_columns = jnp.concatenate([high, middle, low, blank], axis=-1).astype(jnp.bfloat16)
    packed = in_vmem(
        values_body,
        jax.ShapeDtypeStruct((latent_count, 4 * 384), jnp.bfloat16),
        [pltpu.VMEM((4, width, quarter), jnp.bfloat16)],
    )(where, pooled_frames, state_columns, *value_pieces)
    parts = lax.all_gather(packed, "frame")
    z_index = jnp.stack([e // 2]).astype(jnp.int32)
    pooled = in_vmem(combine_body, jax.ShapeDtypeStruct((4, latent_count, 384), jnp.bfloat16))(z_index, parts)

    own_first = e % 2 == 0
    proj_rows = jnp.where(
        own_first, jnp.concatenate([w_proj, proj_other]), jnp.concatenate([proj_other, w_proj])
    )
    proj_rows = jnp.pad(proj_rows, ((0, 384 - 2 * rows), (0, 0)))
    gathered = jnp.concatenate([pooled[0]] + [swap(pooled[d], "expert", 2 * d, 8) for d in (1, 2, 3)])
    partial = jnp.dot(gathered, proj_rows, preferred_element_type=jnp.float32).astype(jnp.bfloat16)
    partial = partial.reshape(4, latent_count, -1)
    x_sum = partial[0].astype(jnp.float32)
    for d in (1, 2, 3):
        x_sum = x_sum + swap(partial[d], "expert", 2 * d, 8).astype(jnp.float32)
    x_part = x_sum.astype(jnp.bfloat16)
    x_float = x_part.astype(jnp.float32)
    part_width = x_part.shape[1]

    expert_total = router.shape[1]
    capacity = latent_count // 2
    pair_ids = expert_ids.reshape(-1)
    onehot = (pair_ids[:, None] == jnp.arange(expert_total, dtype=jnp.int32)[None, :]).astype(jnp.int32)
    earlier_hits = jnp.cumsum(onehot, axis=0) - onehot
    position = jnp.sum(earlier_hits * onehot, axis=-1)
    slot_of = pair_ids * capacity + position
    pair_hit = (
        slot_of[None, :] == jnp.arange(expert_total * capacity, dtype=jnp.int32)[:, None]
    ).astype(jnp.float32)
    select = pair_hit.reshape(-1, latent_count, 2).sum(-1).astype(jnp.bfloat16)
    send_rows = jnp.dot(select, x_part, preferred_element_type=jnp.float32).astype(jnp.bfloat16)
    arrived = lax.all_to_all(
        send_rows.reshape(expert_total, capacity, part_width), "expert", split_axis=0, concat_axis=0, tiled=True
    ).reshape(-1, part_width)

    from_core = swap(arrived, "frame", 1, 4)
    from_y = swap(arrived, "frame", 2, 4)
    from_both = swap(from_y, "frame", 1, 4)
    near = expert_in(where, arrived, from_core, norm_gain, w_gate, w_up, 0)
    hidden = expert_in(where, from_y, from_both, norm_gain, w_gate, w_up, 2, near)
    far_parts = expert_out(where, hidden, w_down, 2)
    chip_far = far_parts[0].astype(jnp.float32) + swap(far_parts[1], "frame", 1, 4).astype(jnp.float32)
    y_sum = swap(chip_far.astype(jnp.bfloat16), "frame", 2, 4)
    near_parts = expert_out(after(where, chip_far), hidden, w_down, 0)
    own_sum = near_parts[0].astype(jnp.float32) + swap(near_parts[1], "frame", 1, 4).astype(jnp.float32)
    summed = (own_sum + y_sum.astype(jnp.float32)).astype(jnp.bfloat16)
    returned = lax.all_to_all(
        summed.reshape(expert_total, capacity, part_width), "expert", split_axis=0, concat_axis=0, tiled=True
    ).reshape(-1, part_width)

    gain_here = lax.dynamic_slice(norm_gain, (f * part_width,), (part_width,)).astype(jnp.float32)
    router_here = lax.dynamic_slice(router, (f * part_width, 0), (part_width, expert_total)).astype(jnp.float32)
    raw = jnp.dot(x_float * gain_here, router_here, precision=lax.Precision.HIGHEST)
    sums = jnp.concatenate([raw, jnp.sum(x_float * x_float, axis=-1, keepdims=True)], axis=-1)
    sums = sums + swap(sums, "frame", 1, 4)
    sums = sums + swap(sums, "frame", 2, 4)
    scale = lax.rsqrt(sums[:, expert_total] / router.shape[0] + EPSILON)
    logits = sums[:, :expert_total] * scale[:, None]
    chosen = jnp.take_along_axis(logits, expert_ids, axis=1)
    gates = jax.nn.softmax(chosen, axis=-1)
    mixing = (pair_hit * gates.reshape(-1)[None, :]).reshape(-1, latent_count, 2).sum(-1)
    moe_part = lax.dot_general(
        mixing, returned.astype(jnp.float32), (((0,), (0,)), ((), ())), precision=lax.Precision.HIGHEST
    )
    return (x_float + moe_part).astype(jnp.bfloat16)


def solution(mesh):
    in_specs = (
        P("expert", "frame", None),
        P("expert"),
        P(),
        P("expert", None),
        P("expert", "frame"),
        P(),
        P(),
        P("expert", None),
        P("expert", None, "frame"),
        P("expert", None, "frame"),
        P("expert", "frame", None),
    )
    out_specs = P("expert", "frame")
    small = mesh.shape["frame"] == 4 and mesh.shape["expert"] == 8
    body = fast_local if small else local
    return jax.shard_map(body, mesh=mesh, in_specs=in_specs, out_specs=out_specs, check_vma=False)
```

```python
import functools
import math

import jax
import jax.numpy as jnp
from jax import lax
from jax.experimental import pallas as pl
from jax.experimental.pallas import tpu as pltpu
from jax.sharding import PartitionSpec as P

HEADS = 16
PATCH = 256


NEG_BIG = -1e30
EPSILON = 1e-05


def joined(value, axis, join):
    pieces = jax.tree.map(lambda part: lax.all_gather(part, axis), value)
    head = jax.tree.map(lambda part: part[0], pieces)
    tail = jax.tree.map(lambda part: part[1:], pieces)
    subtotal, _ = lax.scan(lambda subtotal, piece: (join(subtotal, piece), None), head, tail)
    return subtotal


def rescale(weighted, factor):
    return (weighted.reshape(factor.shape + (-1,)) * factor[..., None]).reshape(weighted.shape)


def combine_parts(earlier, later):
    peak_left, totals_left, weighted_left = earlier
    peak_right, totals_right, weighted_right = later
    peak_both = jnp.maximum(peak_left, peak_right)
    factor_left = jnp.exp(peak_left - peak_both)
    factor_right = jnp.exp(peak_right - peak_both)
    totals_both = totals_left * factor_left + totals_right * factor_right
    weighted_both = rescale(weighted_left, factor_left) + rescale(weighted_right, factor_right)
    return (peak_both, totals_both, weighted_both)


def local(
    frames, frame_counts, latents, w_kv, w_proj, norm_gain, router, expert_ids, w_gate, w_up, w_down
):
    clip_count, frame_tokens, width = frames.shape
    head_count = HEADS
    head_size = width // head_count
    latent_count = latents.shape[0]
    tokens_here = clip_count * latent_count
    flat_frames = frames.reshape(clip_count * frame_tokens, width)
    columns = flat_frames
    kv_sum = jnp.dot(
        columns,
        lax.all_gather(w_kv, "expert", axis=0, tiled=True),
        preferred_element_type=jnp.float32,
    )
    key_value = kv_sum.astype(jnp.bfloat16).reshape(clip_count, frame_tokens, 2 * width)
    key_rows = key_value[:, :, :width].reshape(clip_count, frame_tokens, head_count, head_size)
    value_rows = key_value[:, :, width:].reshape(clip_count, frame_tokens, head_count, head_size)
    queries = latents.reshape(latent_count, head_count, head_size)
    scores = jnp.einsum(
        "lhd,cphd->clhp", queries, key_rows, preferred_element_type=jnp.float32
    ) / math.sqrt(head_size)
    frames_here = frame_tokens // PATCH
    frame_of = (
        lax.axis_index("frame") * frames_here + jnp.arange(frame_tokens, dtype=jnp.int32) // PATCH
    )
    valid = (frame_of[None, :] < frame_counts[:, None])[:, None, None, :]
    masked = jnp.where(valid, scores, NEG_BIG)
    peak = jnp.max(masked, axis=-1)
    expos = jnp.where(valid, jnp.exp(masked - peak[..., None]), 0.0)
    totals = jnp.sum(expos, axis=-1)
    weighted = jnp.einsum("clhp,cphd->clhd", expos, value_rows, preferred_element_type=jnp.float32)
    weighted = weighted.reshape(clip_count, latent_count, width)
    peak_all, totals_all, weighted_all = joined((peak, totals, weighted), "frame", combine_parts)
    pooled = (
        rescale(weighted_all, 1.0 / totals_all).reshape(tokens_here, width).astype(jnp.bfloat16)
    )
    columns = pooled
    x_part = jnp.dot(
        columns,
        lax.all_gather(w_proj, "expert", axis=0, tiled=True),
        preferred_element_type=jnp.float32,
    ).astype(jnp.bfloat16)
    part_width = w_proj.shape[1]
    model_width = router.shape[0]
    gain_all = norm_gain.astype(jnp.float32)
    router_all = router.astype(jnp.float32)
    x_float = x_part.astype(jnp.float32)
    x_whole = lax.all_gather(x_part, "frame", axis=1, tiled=True).astype(jnp.float32)
    squares = jnp.sum(x_whole * x_whole, axis=-1)
    raw_logits = jnp.dot(x_whole * gain_all, router_all, precision=lax.Precision.HIGHEST)
    scale = lax.rsqrt(squares / model_width + EPSILON)
    normed = (x_whole * scale[:, None] * gain_all).astype(jnp.bfloat16)
    logits = raw_logits * scale[:, None]
    chosen = jnp.take_along_axis(logits, expert_ids, axis=1)
    gates = jax.nn.softmax(chosen, axis=-1)
    expert_total = router.shape[1]
    capacity = tokens_here // 2
    pair_ids = expert_ids.reshape(-1)
    onehot = (pair_ids[:, None] == jnp.arange(expert_total, dtype=jnp.int32)[None, :]).astype(
        jnp.int32
    )
    earlier_hits = jnp.cumsum(onehot, axis=0) - onehot
    position = jnp.sum(earlier_hits * onehot, axis=-1)
    slot_of = pair_ids * capacity + position
    pair_hit = (
        slot_of[None, :] == jnp.arange(expert_total * capacity, dtype=jnp.int32)[:, None]
    ).astype(jnp.float32)
    select = pair_hit.reshape(-1, tokens_here, 2).sum(-1).astype(jnp.bfloat16)
    mixing = (pair_hit * gates.reshape(-1)[None, :]).reshape(-1, tokens_here, 2).sum(-1)
    packed = jnp.dot(select, normed, preferred_element_type=jnp.float32).astype(jnp.bfloat16)
    shard_count = lax.axis_size("expert") // expert_total
    row_width = packed.shape[1]
    send_rows = jnp.broadcast_to(
        packed.reshape(expert_total, 1, capacity, row_width),
        (expert_total, shard_count, capacity, row_width),
    )
    send_rows = send_rows.reshape(expert_total * shard_count, capacity, row_width)
    gate_local = w_gate[0]
    up_local = w_up[0]
    down_local = w_down[0]
    arrived = lax.all_to_all(send_rows, "expert", split_axis=0, concat_axis=0, tiled=True)
    flat_rows = arrived.reshape(-1, arrived.shape[-1])
    gate_val = jnp.dot(flat_rows, gate_local, preferred_element_type=jnp.float32)
    up_val = jnp.dot(flat_rows, up_local, preferred_element_type=jnp.float32)
    hidden_rows = (jax.nn.silu(gate_val) * up_val).astype(jnp.bfloat16)
    hidden = hidden_rows.reshape(arrived.shape[0], arrived.shape[1], -1)
    slot_rows = hidden.reshape(-1, hidden.shape[-1])
    columns = down_local
    summed = lax.psum_scatter(
        lax.dot_general(
            columns, slot_rows, (((0,), (1,)), ((), ())), preferred_element_type=jnp.float32
        ).astype(jnp.bfloat16),
        "frame",
        scatter_dimension=0,
        tiled=True,
    )
    outgoing = summed.reshape(part_width, -1, capacity)
    returned = lax.all_to_all(outgoing, "expert", split_axis=1, concat_axis=1, tiled=True)
    per_expert = (
        returned.astype(jnp.float32).reshape(part_width, expert_total, shard_count, capacity).sum(2)
    )
    per_expert = per_expert.reshape(part_width, expert_total * capacity)
    moe_part = jnp.dot(per_expert, mixing, precision=lax.Precision.HIGHEST)
    return (x_float + jnp.transpose(moe_part)).astype(jnp.bfloat16)


def swap(value, axis, bits, size):
    return lax.ppermute(value, axis, [(i, i ^ bits) for i in range(size)])


def hold(value, *earlier):
    if not earlier:
        return value
    there = functools.reduce(jnp.logical_and, [array[(0,) * array.ndim] < jnp.inf for array in earlier])
    return jnp.where(there, value, jnp.zeros((), value.dtype))


PIECES = tuple(tuple((2 * d + e_bit, f_bits) for d in range(4)) for e_bit, f_bits in ((0, 0), (1, 0), (0, 2), (1, 2)))
PLACES = tuple(places for group in PIECES for places in (group, tuple((e, f + 1) for e, f in group)))


def along_z(piece):
    return jnp.stack([piece] + [swap(piece, "expert", 2 * d, 8) for d in (1, 2, 3)])


def spread(column):
    diagonal = [(8 * f + e, 8 * (f ^ 2) + (e ^ 1)) for f in range(4) for e in range(8)]
    by_x = swap(column, "expert", 1, 8)
    by_y = swap(column, "frame", 2, 4)
    by_both = lax.ppermute(column, ("frame", "expert"), diagonal)
    groups = []
    for value in (column, by_x, by_y, by_both):
        groups += [value, swap(value, "frame", 1, 4)]
    return groups, by_both


def each_piece(where, pieces):
    rows = pieces[0].shape[1]
    for places, piece in zip(PLACES, pieces):
        for at, (e_bits, f_bits) in enumerate(places):
            row = pl.multiple_of((where[0] ^ e_bits) * rows, 16)
            yield pl.ds(row, rows), where[1] ^ f_bits, piece[at]


def attend_body(where, frames, *refs):
    pieces, (pooled_frames, states, whole) = refs[: len(PLACES)], refs[-3:]
    for row_range, column, piece in each_piece(where, pieces):
        columns = piece.shape[1]
        whole[row_range, pl.ds(pl.multiple_of(column * columns, 128), columns)] = piece
    tokens = frames.shape[0]
    half = whole.shape[1] // 2
    valid = lax.broadcasted_iota(jnp.int32, (tokens, half), 0) < where[2]
    for part in range(2):
        columns = pl.ds(part * half, half)
        scores = jnp.dot(frames[...], whole[:, columns], preferred_element_type=jnp.float32)
        masked = jnp.where(valid, scores, NEG_BIG)
        peak = jnp.max(masked, axis=0, keepdims=True)
        expos = jnp.where(valid, jnp.exp(masked - peak), 0.0)
        total = jnp.sum(expos, axis=0, keepdims=True)
        some = total > 0.0
        safe = jnp.where(some, total, 1.0)
        weights = (expos * (1.0 / safe)).astype(jnp.bfloat16)
        states[:, columns] = jnp.where(some, peak + jnp.log(safe), NEG_BIG)
        pooled_frames[columns, :] = lax.dot_general(
            weights, frames[...], (((0,), (0,)), ((), ())), preferred_element_type=jnp.float32
        ).astype(jnp.bfloat16)


def values_body(where, pooled_frames, states, *refs):
    pieces, (packed, whole) = refs[: len(PLACES)], refs[len(PLACES) :]
    for row_range, column, piece in each_piece(where, pieces):
        whole[column, row_range, :] = piece
    groups, _, width = whole.shape
    head_size = width // 4
    pairs = pooled_frames.shape[0] // groups
    latents = pairs // 4
    head_of = lax.broadcasted_iota(jnp.int32, (latents, width), 1) // head_size
    for group in range(groups):
        rows = pooled_frames[group * pairs : (group + 1) * pairs, :]
        every = jnp.dot(rows, whole[group], preferred_element_type=jnp.float32)
        own = jnp.zeros((latents, width), jnp.float32)
        for head in range(4):
            own = jnp.where(head_of == head, every[head * latents : (head + 1) * latents, :], own)
        for copy in range(packed.shape[1]):
            packed[group, copy, :, :width] = own.astype(jnp.bfloat16)
            packed[group, copy, :, width:] = states[group]


def combine_body(where, parts, pooled):
    latents = parts.shape[2]
    width = 352
    head_size = width // 4
    head_of = lax.broadcasted_iota(jnp.int32, (latents, width), 1) // head_size
    for turn in range(4):
        logs, values = [], []
        for part in range(4):
            block = parts[where[0] ^ turn, part].astype(jnp.float32)
            state = block[:, width : width + 4] + block[:, width + 4 : width + 8]
            state = state + block[:, width + 8 : width + 12]
            logs.append(state)
            values.append(block[:, :width])
        peak = jnp.maximum(jnp.maximum(logs[0], logs[1]), jnp.maximum(logs[2], logs[3]))
        shares = [jnp.exp(state - peak) for state in logs]
        inverse = 1.0 / (shares[0] + shares[1] + shares[2] + shares[3])
        joined_up = jnp.zeros((latents, width), jnp.float32)
        for share, value in zip(shares, values):
            share = share * inverse
            spread_out = jnp.zeros((latents, width), jnp.float32)
            for head in range(4):
                spread_out = jnp.where(head_of == head, share[:, head : head + 1], spread_out)
            joined_up = joined_up + value * spread_out
        pooled[turn] = jnp.zeros((latents, 384), jnp.bfloat16)
        pooled[turn, :, :width] = joined_up.astype(jnp.bfloat16)


DEPTH = 256
DOWN_WIDTH = 256
SLOTS = 5


def streamed(blocks):
    depth = SLOTS
    copies = [
        [
            pltpu.make_async_copy(source, buffer.at[at % depth], semaphores.at[which, at % depth])
            for which, (source, buffer) in enumerate(zip(sources, buffers))
        ]
        for at, (sources, buffers, semaphores, _) in enumerate(blocks)
    ]
    for group in copies[: depth - 1]:
        for copy in group:
            copy.start()
    for at, (_, buffers, _, work) in enumerate(blocks):
        if at + depth - 1 < len(blocks):
            for copy in copies[at + depth - 1]:
                copy.start()
        for copy in copies[at]:
            copy.wait()
        work(*[buffer.at[at % depth] for buffer in buffers])


def entering(where, bits, rows, gain, gate_w, up_w, gate_sum, up_sum, squares, gate_buffer, up_buffer, semaphores):
    steps = rows[0].shape[1] // DEPTH
    for turn, source in enumerate(rows):
        chunk = where[1] ^ (bits + turn)
        for at in range(steps):
            block_index = chunk * steps + at
            depth_rows = pl.ds(pl.multiple_of(block_index * DEPTH, DEPTH), DEPTH)

            def work(gate_block, up_block, source=source, at=at, block_index=block_index, first=turn + at == 0):
                block = source[:, at * DEPTH : (at + 1) * DEPTH].astype(jnp.float32)
                total = jnp.sum(block * block, axis=1, keepdims=True)
                gained = (block * gain[block_index].astype(jnp.float32)).astype(jnp.bfloat16)
                gate_part = jnp.dot(gained, gate_block[...], preferred_element_type=jnp.float32)
                up_part = jnp.dot(gained, up_block[...], preferred_element_type=jnp.float32)
                if first:
                    squares[...] = jnp.broadcast_to(total, squares.shape)
                    gate_sum[...] = gate_part
                    up_sum[...] = up_part
                else:
                    squares[...] += jnp.broadcast_to(total, squares.shape)
                    gate_sum[...] += gate_part
                    up_sum[...] += up_part

            sources = (gate_w.at[0, depth_rows, :], up_w.at[0, depth_rows, :])
            yield sources, (gate_buffer, up_buffer), semaphores, work


def leaving(where, bits, hidden, down_w, parts, buffer, semaphores):
    steps = parts.shape[2] // DOWN_WIDTH
    for turn, bit in enumerate(bits):
        for at in range(steps):
            start = pl.multiple_of(((where[1] ^ bit) * steps + at) * DOWN_WIDTH, DOWN_WIDTH)

            def work(down_block, turn=turn, at=at):
                parts[turn, :, at * DOWN_WIDTH : (at + 1) * DOWN_WIDTH] = jnp.dot(
                    hidden[...], down_block[...], preferred_element_type=jnp.float32
                ).astype(jnp.bfloat16)

            yield (down_w.at[0, :, pl.ds(start, DOWN_WIDTH)],), (buffer,), semaphores, work


def near_body(where, own, other, gain, gate_w, up_w, gate_sum, up_sum, squares, *scratch):
    streamed(list(entering(where, 0, (own, other), gain, gate_w, up_w, gate_sum, up_sum, squares, *scratch)))


def far_body(where, own, other, gain, gate_w, up_w, gate_in, up_in, squares_in, down_w, hidden, parts, *scratch):
    (gate_sum, up_sum, squares), buffers, (down_buffer, down_semaphores) = scratch[:3], scratch[3:6], scratch[6:]
    blocks = list(entering(where, 2, (own, other), gain, gate_w, up_w, gate_sum, up_sum, squares, *buffers))
    last_work = blocks[-1][3]

    def finish(gate_block, up_block):
        last_work(gate_block, up_block)
        mean = (squares[:, :1] + squares_in[:, :1]) / up_w.shape[1]
        scale = lax.rsqrt(mean + EPSILON)
        gate_val = (gate_sum[...] + gate_in[...]) * scale
        up_val = (up_sum[...] + up_in[...]) * scale
        hidden[...] = (gate_val / (1.0 + jnp.exp(-gate_val)) * up_val).astype(jnp.bfloat16)

    blocks[-1] = (*blocks[-1][:3], finish)
    streamed(blocks + list(leaving(where, (2, 3), hidden, down_w, parts, down_buffer, down_semaphores)))


def last_body(bit, where, hidden, down_w, before, parts, buffer, semaphores):
    streamed(list(leaving(where, (bit,), hidden, down_w, parts, buffer, semaphores)))


def cost(flops, moved):
    return pl.CostEstimate(flops=flops, transcendentals=0, bytes_accessed=moved)


SMEM_SPEC = pl.BlockSpec(memory_space=pltpu.SMEM)
VMEM_SPEC = pl.BlockSpec(memory_space=pltpu.VMEM)
HBM_SPEC = pl.BlockSpec(memory_space=pltpu.HBM)


def weight_buffers(hidden_width):
    block = pltpu.VMEM((SLOTS, DEPTH, hidden_width), jnp.bfloat16)
    return [block, block, pltpu.SemaphoreType.DMA((2, SLOTS))]


def down_buffers(hidden_width):
    return [pltpu.VMEM((SLOTS, hidden_width, DOWN_WIDTH), jnp.bfloat16), pltpu.SemaphoreType.DMA((1, SLOTS))]


def expert_near(where, own, other, gain, gate_w, up_w):
    rows, columns = own.shape
    hidden_width = up_w.shape[2]
    sums = [jax.ShapeDtypeStruct((rows, wide), jnp.float32) for wide in (hidden_width, hidden_width, 128)]
    return pl.pallas_call(
        near_body,
        out_shape=sums,
        in_specs=[SMEM_SPEC] + [VMEM_SPEC] * 3 + [HBM_SPEC] * 2,
        out_specs=[VMEM_SPEC] * 3,
        scratch_shapes=weight_buffers(hidden_width),
        compiler_params=pltpu.CompilerParams(vmem_limit_bytes=20 * 2**20),
        cost_estimate=cost(8 * rows * columns * hidden_width, 8 * columns * hidden_width),
    )(where, own, other, gain, gate_w, up_w)


def expert_far(where, own, other, gain, gate_w, up_w, near, down_w):
    rows, columns = own.shape
    hidden_width = up_w.shape[2]
    return pl.pallas_call(
        far_body,
        out_shape=(
            jax.ShapeDtypeStruct((rows, hidden_width), jnp.bfloat16),
            jax.ShapeDtypeStruct((2, rows, columns), jnp.bfloat16),
        ),
        in_specs=[SMEM_SPEC] + [VMEM_SPEC] * 3 + [HBM_SPEC] * 2 + [VMEM_SPEC] * 3 + [HBM_SPEC],
        out_specs=(VMEM_SPEC, VMEM_SPEC),
        scratch_shapes=[pltpu.VMEM(s.shape, s.dtype) for s in near]
        + weight_buffers(hidden_width)
        + down_buffers(hidden_width),
        compiler_params=pltpu.CompilerParams(vmem_limit_bytes=32 * 2**20),
        cost_estimate=cost(12 * rows * columns * hidden_width, 12 * columns * hidden_width),
    )(where, own, other, gain, gate_w, up_w, *near, down_w)


def expert_last(where, bit, hidden, down_w, before, columns):
    rows, depth = hidden.shape
    return pl.pallas_call(
        functools.partial(last_body, bit),
        out_shape=jax.ShapeDtypeStruct((1, rows, columns), jnp.bfloat16),
        in_specs=[SMEM_SPEC, VMEM_SPEC, HBM_SPEC, pl.BlockSpec(memory_space=pl.ANY)],
        out_specs=VMEM_SPEC,
        scratch_shapes=down_buffers(depth),
        compiler_params=pltpu.CompilerParams(vmem_limit_bytes=16 * 2**20),
        cost_estimate=cost(2 * rows * depth * columns, 2 * depth * columns),
    )(where, hidden, down_w, before)


def in_vmem(body, out_shape, limit, scratch=()):
    space = lambda _: pl.BlockSpec(memory_space=pltpu.VMEM)

    def call(where, *operands):
        return pl.pallas_call(
            body,
            out_shape=out_shape,
            in_specs=[pl.BlockSpec(memory_space=pltpu.SMEM)] + [space(o) for o in operands],
            out_specs=jax.tree.map(space, out_shape),
            scratch_shapes=list(scratch),
            compiler_params=pltpu.CompilerParams(vmem_limit_bytes=limit * 2**20),
        )(where, *operands)

    return call


def fast_local(
    frames, frame_counts, latents, w_kv, w_proj, norm_gain, router, expert_ids, w_gate, w_up, w_down
):
    _, frame_tokens, width = frames.shape
    latent_count = latents.shape[0]
    head_size = width // HEADS
    e, f = lax.axis_index("expert"), lax.axis_index("frame")
    rows = w_kv.shape[0]
    quarter = width // 4
    frames_here = frame_tokens // PATCH
    valid_tokens = jnp.clip((frame_counts[0] - f * frames_here) * PATCH, 0, frame_tokens)
    where = jnp.stack([e, f, valid_tokens]).astype(jnp.int32)

    expert_total = router.shape[1]
    capacity = latent_count // 2
    pair_ids = expert_ids.reshape(-1)
    onehot = (pair_ids[:, None] == jnp.arange(expert_total, dtype=jnp.int32)[None, :]).astype(jnp.int32)
    pair_at = jnp.arange(pair_ids.shape[0], dtype=jnp.int32)
    before = (pair_at[:, None] > pair_at[None, :]).astype(jnp.float32)
    earlier_hits = jnp.dot(before, onehot.astype(jnp.float32)).astype(jnp.int32)
    position = jnp.sum(earlier_hits * onehot, axis=-1)
    slot_of = pair_ids * capacity + position
    pair_hit = (
        slot_of[None, :] == jnp.arange(expert_total * capacity, dtype=jnp.int32)[:, None]
    ).astype(jnp.float32)
    select = pair_hit.reshape(-1, latent_count, 2).sum(-1).astype(jnp.bfloat16)

    head_here = f * 4 + jnp.arange(4, dtype=jnp.int32)
    head_of = jnp.arange(width, dtype=jnp.int32) // head_size
    spaced = jnp.where(
        head_here[:, None, None] == head_of[None, None, :], latents[None], jnp.zeros((), jnp.bfloat16)
    ).reshape(4 * latent_count, width)
    asked = lax.dot_general(
        w_kv[:, :width], spaced, (((1,), (1,)), ((), ())), preferred_element_type=jnp.float32
    )
    asked = (asked / math.sqrt(head_size)).astype(jnp.bfloat16)
    asked_pieces, asked_last = spread(along_z(asked))
    value_piece = lax.dynamic_slice(w_kv, (0, width + f * quarter), (rows, quarter))
    value_column = along_z(value_piece)
    pooled_frames, states = in_vmem(
        attend_body,
        (
            jax.ShapeDtypeStruct((HEADS * latent_count, width), jnp.bfloat16),
            jax.ShapeDtypeStruct((1, HEADS * latent_count), jnp.float32),
        ),
        28,
        [pltpu.VMEM((width, HEADS * latent_count), jnp.bfloat16)],
    )(where, frames[0], *asked_pieces, select)
    value_pieces, value_last = spread(value_column)
    proj_other = swap(hold(w_proj, value_last), "expert", 1, 8)
    by_latent = jnp.transpose(states.reshape(4, 4, latent_count), (0, 2, 1))
    high = lax.reduce_precision(by_latent, 8, 7)
    middle = lax.reduce_precision(by_latent - high, 8, 7)
    low = (by_latent - high) - middle
    blank = jnp.zeros((4, latent_count, 20), jnp.float32)
    state_columns = jnp.concatenate([high, middle, low, blank], axis=-1).astype(jnp.bfloat16)
    packed = in_vmem(
        values_body,
        jax.ShapeDtypeStruct((4, 4, latent_count, 384), jnp.bfloat16),
        20,
        [pltpu.VMEM((4, width, quarter), jnp.bfloat16)],
    )(where, pooled_frames, state_columns, *value_pieces)
    same_x = [[8 * part + 2 * z + x for z in range(4) for part in range(4)] for x in range(2)]
    parts = lax.all_to_all(
        packed.reshape(16 * latent_count, 384), ("frame", "expert"), 0, 0, axis_index_groups=same_x, tiled=True
    ).reshape(4, 4, latent_count, 384)
    z_index = jnp.stack([e // 2]).astype(jnp.int32)
    pooled = in_vmem(combine_body, jax.ShapeDtypeStruct((4, latent_count, 384), jnp.bfloat16), 8)(z_index, parts)

    own_first = e % 2 == 0
    proj_rows = jnp.where(
        own_first, jnp.concatenate([w_proj, proj_other]), jnp.concatenate([proj_other, w_proj])
    )
    proj_rows = jnp.pad(proj_rows, ((0, 384 - 2 * rows), (0, 0)))
    partial = jnp.dot(pooled.reshape(4 * latent_count, 384), proj_rows, preferred_element_type=jnp.float32).astype(jnp.bfloat16)
    partial = partial.reshape(4, latent_count, -1)
    x_sum = partial[0].astype(jnp.float32)
    for d in (1, 2, 3):
        x_sum = x_sum + swap(partial[d], "expert", 2 * d, 8).astype(jnp.float32)
    x_part = x_sum.astype(jnp.bfloat16)
    x_float = x_part.astype(jnp.float32)
    part_width = x_part.shape[1]

    send_rows = jnp.dot(select, x_part, preferred_element_type=jnp.float32).astype(jnp.bfloat16)
    arrived = lax.all_to_all(
        send_rows.reshape(expert_total, capacity, part_width), "expert", split_axis=0, concat_axis=0, tiled=True
    ).reshape(-1, part_width)

    gain = norm_gain.reshape(-1, 1, DEPTH)
    w_gate, w_up, w_down = (pltpu.with_memory_space_constraint(w, pltpu.HBM) for w in (w_gate, w_up, w_down))
    from_core = swap(arrived, "frame", 1, 4)
    from_y = swap(arrived, "frame", 2, 4)
    near = expert_near(where, arrived, from_core, gain, w_gate, w_up)
    from_both = swap(hold(from_y, near[2]), "frame", 1, 4)
    hidden, far_parts = expert_far(where, from_y, from_both, gain, w_gate, w_up, near, w_down)
    chip_far = far_parts[0].astype(jnp.float32) + swap(far_parts[1], "frame", 1, 4).astype(jnp.float32)
    chip_far = chip_far.astype(jnp.bfloat16)
    y_sum = swap(chip_far, "frame", 2, 4)
    for_core = expert_last(where, 1, hidden, w_down, chip_far, part_width)
    for_own = expert_last(where, 0, hidden, w_down, for_core, part_width)
    own_sum = for_own[0].astype(jnp.float32) + swap(for_core[0], "frame", 1, 4).astype(jnp.float32)
    summed = (own_sum + y_sum.astype(jnp.float32)).astype(jnp.bfloat16)
    returned = lax.all_to_all(
        summed.reshape(expert_total, capacity, part_width), "expert", split_axis=0, concat_axis=0, tiled=True
    ).reshape(-1, part_width)

    gain_here = lax.dynamic_slice(norm_gain, (f * part_width,), (part_width,)).astype(jnp.float32)
    router_here = lax.dynamic_slice(router, (f * part_width, 0), (part_width, expert_total)).astype(jnp.float32)
    raw = jnp.dot(x_float * gain_here, router_here, precision=lax.Precision.HIGHEST)
    sums = jnp.concatenate([raw, jnp.sum(x_float * x_float, axis=-1, keepdims=True)], axis=-1)
    sums = hold(sums, chip_far)
    sums = sums + swap(sums, "frame", 1, 4) + swap(sums, "frame", 2, 4) + swap(sums, "frame", 3, 4)
    scale = lax.rsqrt(sums[:, expert_total] / router.shape[0] + EPSILON)
    logits = sums[:, :expert_total] * scale[:, None]
    chosen = jnp.take_along_axis(logits, expert_ids, axis=1)
    gates = jax.nn.softmax(chosen, axis=-1)
    mixing = (pair_hit * gates.reshape(-1)[None, :]).reshape(-1, latent_count, 2).sum(-1)
    moe_part = lax.dot_general(
        mixing, returned.astype(jnp.float32), (((0,), (0,)), ((), ())), precision=lax.Precision.HIGHEST
    )
    return (x_float + moe_part).astype(jnp.bfloat16)


def solution(mesh):
    in_specs = (
        P("expert", "frame", None),
        P("expert"),
        P(),
        P("expert", None),
        P("expert", "frame"),
        P(),
        P(),
        P("expert", None),
        P("expert", None, "frame"),
        P("expert", None, "frame"),
        P("expert", "frame", None),
    )
    out_specs = P("expert", "frame")
    small = mesh.shape["frame"] == 4 and mesh.shape["expert"] == 8
    body = fast_local if small else local
    return jax.shard_map(body, mesh=mesh, in_specs=in_specs, out_specs=out_specs, check_vma=False)
```

```python
import functools
import math

import jax
import jax.numpy as jnp
from jax import lax
from jax.experimental import pallas as pl
from jax.experimental.pallas import tpu as pltpu
from jax.sharding import PartitionSpec as P

HEADS = 16
PATCH = 256


NEG_BIG = -1e30
EPSILON = 1e-05


def joined(value, axis, join):
    pieces = jax.tree.map(lambda part: lax.all_gather(part, axis), value)
    head = jax.tree.map(lambda part: part[0], pieces)
    tail = jax.tree.map(lambda part: part[1:], pieces)
    subtotal, _ = lax.scan(lambda subtotal, piece: (join(subtotal, piece), None), head, tail)
    return subtotal


def rescale(weighted, factor):
    return (weighted.reshape(factor.shape + (-1,)) * factor[..., None]).reshape(weighted.shape)


def combine_parts(earlier, later):
    peak_left, totals_left, weighted_left = earlier
    peak_right, totals_right, weighted_right = later
    peak_both = jnp.maximum(peak_left, peak_right)
    factor_left = jnp.exp(peak_left - peak_both)
    factor_right = jnp.exp(peak_right - peak_both)
    totals_both = totals_left * factor_left + totals_right * factor_right
    weighted_both = rescale(weighted_left, factor_left) + rescale(weighted_right, factor_right)
    return (peak_both, totals_both, weighted_both)


def local(
    frames, frame_counts, latents, w_kv, w_proj, norm_gain, router, expert_ids, w_gate, w_up, w_down
):
    clip_count, frame_tokens, width = frames.shape
    head_count = HEADS
    head_size = width // head_count
    latent_count = latents.shape[0]
    tokens_here = clip_count * latent_count
    flat_frames = frames.reshape(clip_count * frame_tokens, width)
    columns = flat_frames
    kv_sum = jnp.dot(
        columns,
        lax.all_gather(w_kv, "expert", axis=0, tiled=True),
        preferred_element_type=jnp.float32,
    )
    key_value = kv_sum.astype(jnp.bfloat16).reshape(clip_count, frame_tokens, 2 * width)
    key_rows = key_value[:, :, :width].reshape(clip_count, frame_tokens, head_count, head_size)
    value_rows = key_value[:, :, width:].reshape(clip_count, frame_tokens, head_count, head_size)
    queries = latents.reshape(latent_count, head_count, head_size)
    scores = jnp.einsum(
        "lhd,cphd->clhp", queries, key_rows, preferred_element_type=jnp.float32
    ) / math.sqrt(head_size)
    frames_here = frame_tokens // PATCH
    frame_of = (
        lax.axis_index("frame") * frames_here + jnp.arange(frame_tokens, dtype=jnp.int32) // PATCH
    )
    valid = (frame_of[None, :] < frame_counts[:, None])[:, None, None, :]
    masked = jnp.where(valid, scores, NEG_BIG)
    peak = jnp.max(masked, axis=-1)
    expos = jnp.where(valid, jnp.exp(masked - peak[..., None]), 0.0)
    totals = jnp.sum(expos, axis=-1)
    weighted = jnp.einsum("clhp,cphd->clhd", expos, value_rows, preferred_element_type=jnp.float32)
    weighted = weighted.reshape(clip_count, latent_count, width)
    peak_all, totals_all, weighted_all = joined((peak, totals, weighted), "frame", combine_parts)
    pooled = (
        rescale(weighted_all, 1.0 / totals_all).reshape(tokens_here, width).astype(jnp.bfloat16)
    )
    columns = pooled
    x_part = jnp.dot(
        columns,
        lax.all_gather(w_proj, "expert", axis=0, tiled=True),
        preferred_element_type=jnp.float32,
    ).astype(jnp.bfloat16)
    part_width = w_proj.shape[1]
    model_width = router.shape[0]
    gain_all = norm_gain.astype(jnp.float32)
    router_all = router.astype(jnp.float32)
    x_float = x_part.astype(jnp.float32)
    x_whole = lax.all_gather(x_part, "frame", axis=1, tiled=True).astype(jnp.float32)
    squares = jnp.sum(x_whole * x_whole, axis=-1)
    raw_logits = jnp.dot(x_whole * gain_all, router_all, precision=lax.Precision.HIGHEST)
    scale = lax.rsqrt(squares / model_width + EPSILON)
    normed = (x_whole * scale[:, None] * gain_all).astype(jnp.bfloat16)
    logits = raw_logits * scale[:, None]
    chosen = jnp.take_along_axis(logits, expert_ids, axis=1)
    gates = jax.nn.softmax(chosen, axis=-1)
    expert_total = router.shape[1]
    capacity = tokens_here // 2
    pair_ids = expert_ids.reshape(-1)
    onehot = (pair_ids[:, None] == jnp.arange(expert_total, dtype=jnp.int32)[None, :]).astype(
        jnp.int32
    )
    earlier_hits = jnp.cumsum(onehot, axis=0) - onehot
    position = jnp.sum(earlier_hits * onehot, axis=-1)
    slot_of = pair_ids * capacity + position
    pair_hit = (
        slot_of[None, :] == jnp.arange(expert_total * capacity, dtype=jnp.int32)[:, None]
    ).astype(jnp.float32)
    select = pair_hit.reshape(-1, tokens_here, 2).sum(-1).astype(jnp.bfloat16)
    mixing = (pair_hit * gates.reshape(-1)[None, :]).reshape(-1, tokens_here, 2).sum(-1)
    packed = jnp.dot(select, normed, preferred_element_type=jnp.float32).astype(jnp.bfloat16)
    shard_count = lax.axis_size("expert") // expert_total
    row_width = packed.shape[1]
    send_rows = jnp.broadcast_to(
        packed.reshape(expert_total, 1, capacity, row_width),
        (expert_total, shard_count, capacity, row_width),
    )
    send_rows = send_rows.reshape(expert_total * shard_count, capacity, row_width)
    gate_local = w_gate[0]
    up_local = w_up[0]
    down_local = w_down[0]
    arrived = lax.all_to_all(send_rows, "expert", split_axis=0, concat_axis=0, tiled=True)
    flat_rows = arrived.reshape(-1, arrived.shape[-1])
    gate_val = jnp.dot(flat_rows, gate_local, preferred_element_type=jnp.float32)
    up_val = jnp.dot(flat_rows, up_local, preferred_element_type=jnp.float32)
    hidden_rows = (jax.nn.silu(gate_val) * up_val).astype(jnp.bfloat16)
    hidden = hidden_rows.reshape(arrived.shape[0], arrived.shape[1], -1)
    slot_rows = hidden.reshape(-1, hidden.shape[-1])
    columns = down_local
    summed = lax.psum_scatter(
        lax.dot_general(
            columns, slot_rows, (((0,), (1,)), ((), ())), preferred_element_type=jnp.float32
        ).astype(jnp.bfloat16),
        "frame",
        scatter_dimension=0,
        tiled=True,
    )
    outgoing = summed.reshape(part_width, -1, capacity)
    returned = lax.all_to_all(outgoing, "expert", split_axis=1, concat_axis=1, tiled=True)
    per_expert = (
        returned.astype(jnp.float32).reshape(part_width, expert_total, shard_count, capacity).sum(2)
    )
    per_expert = per_expert.reshape(part_width, expert_total * capacity)
    moe_part = jnp.dot(per_expert, mixing, precision=lax.Precision.HIGHEST)
    return (x_float + jnp.transpose(moe_part)).astype(jnp.bfloat16)


def swap(value, axis, bits, size):
    return lax.ppermute(value, axis, [(i, i ^ bits) for i in range(size)])


def hold(value, *earlier):
    if not earlier:
        return value
    there = functools.reduce(jnp.logical_and, [array[(0,) * array.ndim] < jnp.inf for array in earlier])
    return jnp.where(there, value, jnp.zeros((), value.dtype))


PIECES = tuple(tuple((2 * d + e_bit, f_bits) for d in range(4)) for e_bit, f_bits in ((0, 0), (1, 0), (0, 2), (1, 2)))
PLACES = tuple(places for group in PIECES for places in (group, tuple((e, f + 1) for e, f in group)))


def along_z(piece):
    return [piece] + [swap(piece, "expert", 2 * d, 8) for d in (1, 2, 3)]


def spread(column):
    diagonal = [(8 * f + e, 8 * (f ^ 2) + (e ^ 1)) for f in range(4) for e in range(8)]
    by_x = swap(column, "expert", 1, 8)
    by_y = swap(column, "frame", 2, 4)
    by_both = lax.ppermute(column, ("frame", "expert"), diagonal)
    groups = []
    for value in (column, by_x, by_y, by_both):
        groups += [value, swap(value, "frame", 1, 4)]
    return groups


def each_piece(where, pieces):
    rows = pieces[0].shape[1]
    for places, piece in zip(PLACES, pieces):
        for at, (e_bits, f_bits) in enumerate(places):
            row = pl.multiple_of((where[0] ^ e_bits) * rows, 16)
            yield pl.ds(row, rows), f_bits, piece[at]


def attend_body(where, frames, *refs):
    pieces, (keep, give, states, whole) = refs[: len(PLACES)], refs[-4:]
    for row_range, bits, piece in each_piece(where, pieces):
        columns = piece.shape[1]
        first = (bits % 2 * 2 + bits // 2) * columns
        whole[row_range, first : first + columns] = piece
    tokens = frames.shape[0]
    half = whole.shape[1] // 2
    valid = lax.broadcasted_iota(jnp.int32, (tokens, half), 0) < where[2]
    for part, out in ((1, give), (0, keep)):
        scores = jnp.dot(frames[...], whole[:, part * half : (part + 1) * half], preferred_element_type=jnp.float32)
        masked = jnp.where(valid, scores, NEG_BIG)
        peak = jnp.max(masked, axis=0, keepdims=True)
        expos = jnp.where(valid, jnp.exp(masked - peak), 0.0)
        total = jnp.sum(expos, axis=0, keepdims=True)
        some = total > 0.0
        safe = jnp.where(some, total, 1.0)
        weights = (expos * (1.0 / safe)).astype(jnp.bfloat16)
        state = jnp.where(some, peak + jnp.log(safe), NEG_BIG)
        pairs = states.shape[1]
        for at in range(2):
            bits = part + 2 * at
            states[bits : bits + 1, :] = state[:, at * pairs : (at + 1) * pairs]
        out[...] = lax.dot_general(
            weights, frames[...], (((0,), (0,)), ((), ())), preferred_element_type=jnp.float32
        ).astype(jnp.bfloat16)


def pair_body(keep, got, own_states, core_states, y_states, both_states, mine, theirs):
    pairs = own_states.shape[1]
    all_states = (own_states, core_states, y_states, both_states)
    for at, out in ((1, theirs), (0, mine)):
        logs = [states[(2 * at) ^ bits : ((2 * at) ^ bits) + 1, :] for bits, states in enumerate(all_states)]
        peak = jnp.maximum(jnp.maximum(logs[0], logs[1]), jnp.maximum(logs[2], logs[3]))
        shares = [jnp.exp(state - peak) for state in logs]
        inverse = 1.0 / (shares[0] + shares[1] + shares[2] + shares[3])
        scaled = []
        for share, part in ((shares[0], keep), (shares[1], got)):
            column = jnp.transpose(jnp.broadcast_to(share * inverse, (pairs, pairs)))[:, :1]
            scaled.append(part[at * pairs : (at + 1) * pairs, :].astype(jnp.float32) * column)
        out[...] = (scaled[0] + scaled[1]).astype(jnp.bfloat16)


def values_body(where, mine, other, column, by_x, pooled, whole):
    rows = column.shape[1]
    width = whole.shape[1]
    for bit, pieces in ((0, column), (1, by_x)):
        for d in range(4):
            row = pl.multiple_of((where[0] ^ (2 * d + bit)) * rows, 16)
            whole[pl.ds(row, rows), :] = pieces[d]
    head_size = width // 4
    latents = mine.shape[0] // 4
    head_of = lax.broadcasted_iota(jnp.int32, (latents, width), 1) // head_size
    both = (mine[...].astype(jnp.float32) + other[...].astype(jnp.float32)).astype(jnp.bfloat16)
    every = jnp.dot(both, whole[...], preferred_element_type=jnp.float32)
    own = jnp.zeros((latents, width), jnp.float32)
    for head in range(4):
        own = jnp.where(head_of == head, every[head * latents : (head + 1) * latents, :], own)
    pooled[...] = jnp.zeros_like(pooled)
    pooled[:, :width] = own.astype(jnp.bfloat16)


def project_body(where, *refs):
    pooled, (own_rows, other_rows, partial, gathered, weight) = refs[:4], refs[4:]
    rows = own_rows.shape[0]
    x_bit = where[0] % 2
    weight[pl.ds(pl.multiple_of(x_bit * rows, 16), rows), :] = own_rows[...]
    weight[pl.ds(pl.multiple_of((1 - x_bit) * rows, 16), rows), :] = other_rows[...]
    spare = weight.shape[0] - 2 * rows
    weight[2 * rows :, :] = jnp.zeros((spare, weight.shape[1]), jnp.bfloat16)
    latents = partial.shape[1]
    for bits in range(4):
        turn = where[0] // 2 ^ where[1] ^ bits
        gathered[pl.ds(pl.multiple_of(turn * latents, latents), latents), :] = pooled[bits][...]
    product = jnp.dot(gathered[...], weight[...], preferred_element_type=jnp.float32).astype(jnp.bfloat16)
    for turn in range(4):
        partial[turn] = product[turn * latents : (turn + 1) * latents, :]


DEPTH = 256
DOWN_WIDTH = 256
SLOTS = 5


def streamed(blocks):
    depth = SLOTS
    copies = [
        [
            pltpu.make_async_copy(source, buffer.at[at % depth], semaphores.at[which, at % depth])
            for which, (source, buffer) in enumerate(zip(sources, buffers))
        ]
        for at, (sources, buffers, semaphores, _) in enumerate(blocks)
    ]
    for group in copies[: depth - 1]:
        for copy in group:
            copy.start()
    for at, (_, buffers, _, work) in enumerate(blocks):
        if at + depth - 1 < len(blocks):
            for copy in copies[at + depth - 1]:
                copy.start()
        for copy in copies[at]:
            copy.wait()
        work(*[buffer.at[at % depth] for buffer in buffers])


def entering(where, bits, rows, gain, gate_w, up_w, gate_sum, up_sum, squares, gate_buffer, up_buffer, semaphores):
    steps = rows[0].shape[1] // DEPTH
    for turn, source in enumerate(rows):
        chunk = where[1] ^ (bits + turn)
        for at in range(steps):
            block_index = chunk * steps + at
            depth_rows = pl.ds(pl.multiple_of(block_index * DEPTH, DEPTH), DEPTH)

            def work(gate_block, up_block, source=source, at=at, block_index=block_index, first=turn + at == 0):
                block = source[:, at * DEPTH : (at + 1) * DEPTH].astype(jnp.float32)
                total = jnp.sum(block * block, axis=1, keepdims=True)
                gained = (block * gain[block_index].astype(jnp.float32)).astype(jnp.bfloat16)
                gate_part = jnp.dot(gained, gate_block[...], preferred_element_type=jnp.float32)
                up_part = jnp.dot(gained, up_block[...], preferred_element_type=jnp.float32)
                if first:
                    squares[...] = jnp.broadcast_to(total, squares.shape)
                    gate_sum[...] = gate_part
                    up_sum[...] = up_part
                else:
                    squares[...] += jnp.broadcast_to(total, squares.shape)
                    gate_sum[...] += gate_part
                    up_sum[...] += up_part

            sources = (gate_w.at[0, depth_rows, :], up_w.at[0, depth_rows, :])
            yield sources, (gate_buffer, up_buffer), semaphores, work


def leaving(where, bits, hidden, down_w, parts, buffer, semaphores):
    steps = parts.shape[2] // DOWN_WIDTH
    for turn, bit in enumerate(bits):
        for at in range(steps):
            start = pl.multiple_of(((where[1] ^ bit) * steps + at) * DOWN_WIDTH, DOWN_WIDTH)

            def work(down_block, turn=turn, at=at):
                parts[turn, :, at * DOWN_WIDTH : (at + 1) * DOWN_WIDTH] = jnp.dot(
                    hidden[...], down_block[...], preferred_element_type=jnp.float32
                ).astype(jnp.bfloat16)

            yield (down_w.at[0, :, pl.ds(start, DOWN_WIDTH)],), (buffer,), semaphores, work


def near_body(where, own, other, gain, gate_w, up_w, gate_sum, up_sum, squares, *scratch):
    streamed(list(entering(where, 0, (own, other), gain, gate_w, up_w, gate_sum, up_sum, squares, *scratch)))


def far_body(where, own, other, gain, gate_w, up_w, gate_in, up_in, squares_in, down_w, hidden, parts, *scratch):
    (gate_sum, up_sum, squares), buffers, (down_buffer, down_semaphores) = scratch[:3], scratch[3:6], scratch[6:]
    blocks = list(entering(where, 2, (own, other), gain, gate_w, up_w, gate_sum, up_sum, squares, *buffers))
    last_work = blocks[-1][3]

    def finish(gate_block, up_block):
        last_work(gate_block, up_block)
        mean = (squares[:, :1] + squares_in[:, :1]) / up_w.shape[1]
        scale = lax.rsqrt(mean + EPSILON)
        gate_val = (gate_sum[...] + gate_in[...]) * scale
        up_val = (up_sum[...] + up_in[...]) * scale
        hidden[...] = (gate_val / (1.0 + jnp.exp(-gate_val)) * up_val).astype(jnp.bfloat16)

    blocks[-1] = (*blocks[-1][:3], finish)
    streamed(blocks + list(leaving(where, (2, 3), hidden, down_w, parts, down_buffer, down_semaphores)))


def last_body(bit, where, hidden, down_w, before, parts, buffer, semaphores):
    streamed(list(leaving(where, (bit,), hidden, down_w, parts, buffer, semaphores)))


def cost(flops, moved):
    return pl.CostEstimate(flops=flops, transcendentals=0, bytes_accessed=moved)


SMEM_SPEC = pl.BlockSpec(memory_space=pltpu.SMEM)
VMEM_SPEC = pl.BlockSpec(memory_space=pltpu.VMEM)
HBM_SPEC = pl.BlockSpec(memory_space=pltpu.HBM)
ANY_SPEC = pl.BlockSpec(memory_space=pl.ANY)


def weight_buffers(hidden_width):
    block = pltpu.VMEM((SLOTS, DEPTH, hidden_width), jnp.bfloat16)
    return [block, block, pltpu.SemaphoreType.DMA((2, SLOTS))]


def down_buffers(hidden_width):
    return [pltpu.VMEM((SLOTS, hidden_width, DOWN_WIDTH), jnp.bfloat16), pltpu.SemaphoreType.DMA((1, SLOTS))]


def expert_near(where, own, other, gain, gate_w, up_w):
    rows, columns = own.shape
    hidden_width = up_w.shape[2]
    sums = [jax.ShapeDtypeStruct((rows, wide), jnp.float32) for wide in (hidden_width, hidden_width, 128)]
    return pl.pallas_call(
        near_body,
        out_shape=sums,
        in_specs=[SMEM_SPEC] + [VMEM_SPEC] * 3 + [HBM_SPEC] * 2,
        out_specs=[VMEM_SPEC] * 3,
        scratch_shapes=weight_buffers(hidden_width),
        compiler_params=pltpu.CompilerParams(vmem_limit_bytes=20 * 2**20),
        cost_estimate=cost(8 * rows * columns * hidden_width, 8 * columns * hidden_width),
    )(where, own, other, gain, gate_w, up_w)


def expert_far(where, own, other, gain, gate_w, up_w, near, down_w):
    rows, columns = own.shape
    hidden_width = up_w.shape[2]
    return pl.pallas_call(
        far_body,
        out_shape=(
            jax.ShapeDtypeStruct((rows, hidden_width), jnp.bfloat16),
            jax.ShapeDtypeStruct((2, rows, columns), jnp.bfloat16),
        ),
        in_specs=[SMEM_SPEC] + [VMEM_SPEC] * 3 + [HBM_SPEC] * 2 + [VMEM_SPEC] * 3 + [HBM_SPEC],
        out_specs=(VMEM_SPEC, VMEM_SPEC),
        scratch_shapes=[pltpu.VMEM(s.shape, s.dtype) for s in near]
        + weight_buffers(hidden_width)
        + down_buffers(hidden_width),
        compiler_params=pltpu.CompilerParams(vmem_limit_bytes=32 * 2**20),
        cost_estimate=cost(12 * rows * columns * hidden_width, 12 * columns * hidden_width),
    )(where, own, other, gain, gate_w, up_w, *near, down_w)


def expert_last(where, bit, hidden, down_w, before, columns):
    rows, depth = hidden.shape
    return pl.pallas_call(
        functools.partial(last_body, bit),
        out_shape=jax.ShapeDtypeStruct((1, rows, columns), jnp.bfloat16),
        in_specs=[SMEM_SPEC, VMEM_SPEC, HBM_SPEC, pl.BlockSpec(memory_space=pl.ANY)],
        out_specs=VMEM_SPEC,
        scratch_shapes=down_buffers(depth),
        compiler_params=pltpu.CompilerParams(vmem_limit_bytes=16 * 2**20),
        cost_estimate=cost(2 * rows * depth * columns, 2 * depth * columns),
    )(where, hidden, down_w, before)


def in_vmem(body, out_shape, limit, scratch=()):
    space = lambda _: pl.BlockSpec(memory_space=pltpu.VMEM)

    def call(*operands, before=()):
        return pl.pallas_call(
            body,
            out_shape=out_shape,
            in_specs=[SMEM_SPEC if o.ndim == 1 else space(o) for o in operands] + [ANY_SPEC] * len(before),
            out_specs=jax.tree.map(space, out_shape),
            scratch_shapes=list(scratch),
            compiler_params=pltpu.CompilerParams(vmem_limit_bytes=limit * 2**20),
        )(*operands, *before)

    return call


def fast_local(
    frames, frame_counts, latents, w_kv, w_proj, norm_gain, router, expert_ids, w_gate, w_up, w_down
):
    _, frame_tokens, width = frames.shape
    latent_count = latents.shape[0]
    head_size = width // HEADS
    e, f = lax.axis_index("expert"), lax.axis_index("frame")
    rows = w_kv.shape[0]
    quarter = width // 4
    frames_here = frame_tokens // PATCH
    valid_tokens = jnp.clip((frame_counts[0] - f * frames_here) * PATCH, 0, frame_tokens)
    where = jnp.stack([e, f, valid_tokens]).astype(jnp.int32)

    expert_total = router.shape[1]
    capacity = latent_count // 2
    pair_ids = expert_ids.reshape(-1)
    onehot = (pair_ids[:, None] == jnp.arange(expert_total, dtype=jnp.int32)[None, :]).astype(jnp.int32)
    pair_at = jnp.arange(pair_ids.shape[0], dtype=jnp.int32)
    before = (pair_at[:, None] > pair_at[None, :]).astype(jnp.float32)
    earlier_hits = jnp.dot(before, onehot.astype(jnp.float32)).astype(jnp.int32)
    position = jnp.sum(earlier_hits * onehot, axis=-1)
    slot_of = pair_ids * capacity + position
    pair_hit = (
        slot_of[None, :] == jnp.arange(expert_total * capacity, dtype=jnp.int32)[:, None]
    ).astype(jnp.float32)
    select = pair_hit.reshape(-1, latent_count, 2).sum(-1).astype(jnp.bfloat16)

    head_here = f * 4 + jnp.arange(4, dtype=jnp.int32)
    head_of = jnp.arange(width, dtype=jnp.int32) // head_size
    spaced = jnp.where(
        head_here[:, None, None] == head_of[None, None, :], latents[None], jnp.zeros((), jnp.bfloat16)
    ).reshape(4 * latent_count, width)
    asked = lax.dot_general(
        w_kv[:, :width], spaced, (((1,), (1,)), ((), ())), preferred_element_type=jnp.float32
    )
    asked = (asked / math.sqrt(head_size)).astype(jnp.bfloat16)
    asked_along = along_z(asked)
    asked_column = jnp.stack(asked_along)
    asked_pieces = spread(asked_column)
    value_piece = lax.dynamic_slice(w_kv, (0, width + f * quarter), (rows, quarter))
    value_column = jnp.stack(along_z(hold(value_piece, asked_along[1], asked_along[3])))
    value_x = swap(value_column, "expert", 1, 8)
    proj_other = swap(hold(w_proj, value_x), "expert", 1, 8)

    half = jax.ShapeDtypeStruct((HEADS // 2 * latent_count, width), jnp.bfloat16)
    piece = jax.ShapeDtypeStruct((4 * latent_count, width), jnp.bfloat16)
    keep, give, states = in_vmem(
        attend_body,
        (half, half, jax.ShapeDtypeStruct((4, 4 * latent_count), jnp.float32)),
        28,
        [pltpu.VMEM((width, HEADS * latent_count), jnp.bfloat16)],
    )(where, frames[0], *asked_pieces, before=(select, value_column))
    got = swap(give, "frame", 1, 4)
    other_states = [swap(states, "frame", bits, 4) for bits in (1, 2, 3)]
    mine, theirs = in_vmem(pair_body, (piece, piece), 16)(keep, got, states, *other_states)
    from_across = swap(theirs, "frame", 2, 4)
    pooled = in_vmem(
        values_body,
        jax.ShapeDtypeStruct((latent_count, 384), jnp.bfloat16),
        12,
        [pltpu.VMEM((width, quarter), jnp.bfloat16)],
    )(where, mine, from_across, value_column, value_x)
    pooled_here = [
        lax.ppermute(
            pooled,
            ("frame", "expert"),
            [(8 * f + 2 * z + x, 8 * (z ^ bits) + 2 * f + x) for f in range(4) for z in range(4) for x in range(2)],
        )
        for bits in range(4)
    ]
    partial = in_vmem(
        project_body,
        jax.ShapeDtypeStruct((4, latent_count, w_proj.shape[1]), jnp.bfloat16),
        16,
        [pltpu.VMEM((4 * latent_count, 384), jnp.bfloat16), pltpu.VMEM((384, w_proj.shape[1]), jnp.bfloat16)],
    )(where, *pooled_here, w_proj, proj_other)
    x_sum = partial[0].astype(jnp.float32)
    for d in (1, 2, 3):
        x_sum = x_sum + swap(partial[d], "expert", 2 * d, 8).astype(jnp.float32)
    x_part = x_sum.astype(jnp.bfloat16)
    x_float = x_part.astype(jnp.float32)
    part_width = x_part.shape[1]

    send_rows = jnp.dot(select, x_part, preferred_element_type=jnp.float32).astype(jnp.bfloat16)
    arrived = lax.all_to_all(
        send_rows.reshape(expert_total, capacity, part_width), "expert", split_axis=0, concat_axis=0, tiled=True
    ).reshape(-1, part_width)

    gain = norm_gain.reshape(-1, 1, DEPTH)
    w_gate, w_up, w_down = (pltpu.with_memory_space_constraint(w, pltpu.HBM) for w in (w_gate, w_up, w_down))
    from_core = swap(arrived, "frame", 1, 4)
    from_y = swap(arrived, "frame", 2, 4)
    near = expert_near(where, arrived, from_core, gain, w_gate, w_up)
    from_both = swap(hold(from_y, near[2]), "frame", 1, 4)
    hidden, far_parts = expert_far(where, from_y, from_both, gain, w_gate, w_up, near, w_down)
    chip_far = far_parts[0].astype(jnp.float32) + swap(far_parts[1], "frame", 1, 4).astype(jnp.float32)
    chip_far = chip_far.astype(jnp.bfloat16)
    y_sum = swap(chip_far, "frame", 2, 4)
    for_core = expert_last(where, 1, hidden, w_down, chip_far, part_width)
    for_own = expert_last(where, 0, hidden, w_down, for_core, part_width)
    own_sum = for_own[0].astype(jnp.float32) + swap(for_core[0], "frame", 1, 4).astype(jnp.float32)
    summed = (own_sum + y_sum.astype(jnp.float32)).astype(jnp.bfloat16)
    returned = lax.all_to_all(
        summed.reshape(expert_total, capacity, part_width), "expert", split_axis=0, concat_axis=0, tiled=True
    ).reshape(-1, part_width)

    gain_here = lax.dynamic_slice(norm_gain, (f * part_width,), (part_width,)).astype(jnp.float32)
    router_here = lax.dynamic_slice(router, (f * part_width, 0), (part_width, expert_total)).astype(jnp.float32)
    raw = jnp.dot(x_float * gain_here, router_here, precision=lax.Precision.HIGHEST)
    sums = jnp.concatenate([raw, jnp.sum(x_float * x_float, axis=-1, keepdims=True)], axis=-1)
    sums = hold(sums, chip_far)
    sums = sums + swap(sums, "frame", 1, 4) + swap(sums, "frame", 2, 4) + swap(sums, "frame", 3, 4)
    scale = lax.rsqrt(sums[:, expert_total] / router.shape[0] + EPSILON)
    logits = sums[:, :expert_total] * scale[:, None]
    chosen = jnp.take_along_axis(logits, expert_ids, axis=1)
    gates = jax.nn.softmax(chosen, axis=-1)
    mixing = (pair_hit * gates.reshape(-1)[None, :]).reshape(-1, latent_count, 2).sum(-1)
    moe_part = lax.dot_general(
        mixing, returned.astype(jnp.float32), (((0,), (0,)), ((), ())), precision=lax.Precision.HIGHEST
    )
    return (x_float + moe_part).astype(jnp.bfloat16)


def solution(mesh):
    in_specs = (
        P("expert", "frame", None),
        P("expert"),
        P(),
        P("expert", None),
        P("expert", "frame"),
        P(),
        P(),
        P("expert", None),
        P("expert", None, "frame"),
        P("expert", None, "frame"),
        P("expert", "frame", None),
    )
    out_specs = P("expert", "frame")
    small = mesh.shape["frame"] == 4 and mesh.shape["expert"] == 8
    body = fast_local if small else local
    return jax.shard_map(body, mesh=mesh, in_specs=in_specs, out_specs=out_specs, check_vma=False)
```
